32 devices in a mesh: wide: 8 (over z, core), narrow: 4 (over y, x).
Axes of the slice: x: 2, y: 2, z: 4, core: 2. Of those that a mesh axis runs over, the one named last changes fastest.
Arguments:
- tokens: bfloat16 [8192, 2304], P(('wide', 'narrow')), may hold values from -6 to 6
- target: bfloat16 [8192, 2304], P(('wide', 'narrow')), may hold values from -6 to 6
- combine: bfloat16 [8192], P(('wide', 'narrow')), may hold values from 0.25 to 1
- filled: int32 [8], P('wide'), may hold values from 512 to 1024, as said below
- w_gate: bfloat16 [2304, 2048], P(None, 'narrow'), may hold values from -0.125 to 0.125
- w_up: bfloat16 [2304, 2048], P(None, 'narrow'), may hold values from -0.125 to 0.125
- w_down: bfloat16 [2048, 2304], P('narrow'), may hold values from -0.125 to 0.125
- momentum: float32 [8, 2048, 2304], P('wide', 'narrow'), may hold values from -6 to 6
Outputs:
- momentum_out: float32 [8, 2048, 2304], P('wide', 'narrow')
- update: bfloat16 [2048, 2304], P('narrow')
The draws below stay inside these ranges and needn't reach their ends.
Inputs may be any that keep to these rules, and one draw needn't show every extreme that they name: `filled`: rows of a replica at or after its count are empty buffer slots; some replica's buffer is full in every draw.
All inputs are finite; a program needn't handle non-finite values.
Results may differ from the reference program's by a relative error of at most 0.015.
Values may be sent and summed in bfloat16 or wider, within the bound.
A program may use at most 128 MiB of HBM per device.

```python
import math
import jax
import jax.numpy as jnp
from jax import lax

D = 2304
F = 2048
SPAN = 64
BAND = 16
TOK_DEV = 1024
TOKENS = 8192
N_WIDE = 8
N_NARROW = 4


def draw_filled(key, part):
    counts = jax.random.randint(key, (N_WIDE,), TOK_DEV // 2, TOK_DEV + 1)
    full_index = jax.random.randint(jax.random.fold_in(key, 11), (), 0, N_WIDE)
    return jnp.where(jnp.arange(N_WIDE) == full_index, TOK_DEV, counts).astype(jnp.int32)


def block_scale(key, shape, cuts, smallest, top_value):
    level = 1.0
    for axis_at, parts in cuts:
        heights = jax.random.uniform(jax.random.fold_in(jax.random.fold_in(key, 6), axis_at), (parts,), jnp.float32, smallest / len(cuts), top_value / len(cuts))
        level = level * jnp.repeat(jnp.exp(heights), shape[axis_at] // parts).reshape((-1,) + (1,) * (len(shape) - 1 - axis_at))
    return level


def gaussian(rng, shape, scale, limit, cuts=(), held_as=jnp.bfloat16):
    result = jax.random.normal(rng, shape, jnp.float32) * scale
    if len(cuts) > 0:
        result = block_scale(rng, shape, cuts, -0.22, 0.18) * result
    return jnp.clip(result, min=-limit, max=limit).astype(held_as)


def setup_inputs(seed: int = 0) -> dict:
    splits = jax.random.split(jax.random.key(seed), 9)
    tokens = gaussian(splits[0], (TOKENS, D), 1.0, 6.0, ((0, 32),))
    target = gaussian(splits[1], (TOKENS, D), 1.0, 6.0, ((0, 32),))
    combine = jnp.clip(0.25 + 0.75 * jax.random.uniform(splits[2], (TOKENS,), jnp.float32) ** block_scale(splits[2], (TOKENS,), ((0, 32),), -0.2, 0.2), 0.25, 1.0).astype(jnp.bfloat16)
    filled = draw_filled(jax.random.fold_in(splits[8], 71), 0)
    w_gate = gaussian(splits[4], (D, F), D ** -0.5, 0.125, ((1, 4),))
    w_up = gaussian(splits[5], (D, F), D ** -0.5, 0.125, ((1, 4),))
    w_down = gaussian(splits[6], (F, D), F ** -0.5, 0.125, ((0, 4),))
    momentum = gaussian(splits[7], (N_WIDE, F, D), 1.0, 6.0, ((0, 8), (1, 4)), jnp.float32)
    return dict(tokens=tokens, target=target, combine=combine, filled=filled, w_gate=w_gate, w_up=w_up, w_down=w_down, momentum=momentum)


def cosine_table():
    freq_index = jnp.arange(BAND)[:, None].astype(jnp.float32)
    cell_index = jnp.arange(SPAN)[None, :].astype(jnp.float32)
    factor = jnp.where(freq_index == 0, math.sqrt(1.0 / SPAN), math.sqrt(2.0 / SPAN))
    return factor * jnp.cos(math.pi * (2.0 * cell_index + 1.0) * freq_index / (2.0 * SPAN))

def encode(matrix, table):
    height, breadth = matrix.shape
    blocks = matrix.reshape(height // SPAN, SPAN, breadth // SPAN, SPAN)
    return jnp.einsum('kn,anbm,lm->abkl', table, blocks, table, precision=lax.Precision.HIGHEST)

def decode(band_coef, table):
    across, down_count = (band_coef.shape[0], band_coef.shape[1])
    blocks = jnp.einsum('kn,abkl,lm->anbm', table, band_coef, table, precision=lax.Precision.HIGHEST)
    return blocks.reshape(across * SPAN, down_count * SPAN)

def reference(tokens, target, combine, filled, w_gate, w_up, w_down, momentum):
    table = cosine_table()
    factor = 1.0 / math.sqrt(TOK_DEV)
    group_units = F // N_NARROW

    def replica(index):
        first_row = index * TOK_DEV
        rows_in = lax.dynamic_slice_in_dim(tokens, first_row, TOK_DEV, 0)
        rows_target = lax.dynamic_slice_in_dim(target, first_row, TOK_DEV, 0).astype(jnp.float32)
        weight = lax.dynamic_slice_in_dim(combine, first_row, TOK_DEV, 0).astype(jnp.float32)[:, None]
        gate_proj = jnp.dot(rows_in, w_gate, preferred_element_type=jnp.float32)
        up_proj = jnp.dot(rows_in, w_up, preferred_element_type=jnp.float32)
        hidden = (jax.nn.silu(gate_proj) * up_proj).astype(jnp.bfloat16)
        grouped = jnp.einsum('tnf,nfd->ntd', hidden.reshape(TOK_DEV, N_NARROW, group_units).astype(jnp.float32), w_down.reshape(N_NARROW, group_units, D).astype(jnp.float32))
        summed = lax.optimization_barrier(jnp.sum(lax.optimization_barrier(grouped.astype(jnp.bfloat16)).astype(jnp.float32), axis=0))
        expert_out = weight * summed
        live_rows = jnp.arange(TOK_DEV, dtype=jnp.int32) < filled[index]
        error = jnp.where(live_rows[:, None], weight * (expert_out - rows_target), 0.0).astype(jnp.bfloat16)
        grad = jnp.dot(hidden.T, error, preferred_element_type=jnp.float32) * factor
        moved = 0.999 * momentum[index] + grad
        band_coef = encode(moved, table)
        residue = moved - decode(band_coef, table)
        return (residue, band_coef)
    momentum_out, bands = lax.map(replica, jnp.arange(N_WIDE, dtype=jnp.int32))
    update = (decode(lax.optimization_barrier(jnp.sum(bands, axis=0)), table) / N_WIDE).astype(jnp.bfloat16)
    return (momentum_out, update)
```

```python
import functools
import math

import jax
import jax.numpy as jnp
from jax import lax
from jax.experimental import pallas as pl
from jax.experimental.pallas import tpu as pltpu
from jax.sharding import PartitionSpec as P

SPAN = 64
BAND = 16
TILE = 256
BF = jnp.bfloat16
F32 = jnp.float32


def block_table(blocks):
    shape = (blocks * BAND, blocks * SPAN)
    row = lax.broadcasted_iota(jnp.int32, shape, 0)
    col = lax.broadcasted_iota(jnp.int32, shape, 1)
    freq = (row % BAND).astype(F32)
    cell = (col % SPAN).astype(F32)
    factor = jnp.where(row % BAND == 0, math.sqrt(1.0 / SPAN), math.sqrt(2.0 / SPAN))
    value = factor * jnp.cos(math.pi * (2.0 * cell + 1.0) * freq / (2.0 * SPAN))
    return jnp.where(row // BAND == col // SPAN, value, 0.0)


def halves(value):
    high = value.astype(BF)
    return high, (value - high.astype(F32)).astype(BF)


def dot3(left, right, contract):
    dims = (((contract[0],), (contract[1],)), ((), ()))
    dot = functools.partial(lax.dot_general, dimension_numbers=dims, preferred_element_type=F32)
    return dot(left[0], right[0]) + (dot(left[1], right[0]) + dot(left[0], right[1]))


def decode_tile(band_t, row_table, col_table):
    upper = dot3(halves(band_t), row_table, (1, 0))
    return dot3(halves(upper), col_table, (0, 0))


def grad_kernel(factor, hidden, error, momentum, row_h, row_l, col_h, col_l, residue, band):
    row_table = (row_h[...], row_l[...])
    col_table = (col_h[...], col_l[...])
    grad = lax.dot_general(
        hidden[...], error[...], (((0,), (0,)), ((), ())), preferred_element_type=F32
    )
    moved = 0.999 * momentum[0] + factor * grad
    squeezed = dot3(row_table, halves(moved), (1, 0))
    band_t = dot3(col_table, halves(squeezed), (1, 1))
    band[...] = band_t.astype(BF)
    residue[0] = moved - decode_tile(band_t, row_table, col_table)


def grad_step(hidden, error, momentum, tables, factor):
    rows, units = hidden.shape
    width = error.shape[1]
    tiles = width // TILE
    kept = units // SPAN * BAND
    kept_t = TILE // SPAN * BAND
    whole = lambda a: pl.BlockSpec(a.shape, lambda i: (0, 0))
    return pl.pallas_call(
        functools.partial(grad_kernel, factor),
        grid=(tiles,),
        in_specs=[
            whole(hidden),
            pl.BlockSpec((rows, TILE), lambda i: (0, i)),
            pl.BlockSpec((1, units, TILE), lambda i: (0, 0, i)),
        ]
        + [whole(t) for t in tables],
        out_specs=[
            pl.BlockSpec((1, units, TILE), lambda i: (0, 0, i)),
            pl.BlockSpec((kept_t, kept), lambda i: (i, 0)),
        ],
        out_shape=[
            jax.ShapeDtypeStruct((1, units, width), F32),
            jax.ShapeDtypeStruct((tiles * kept_t, kept), BF),
        ],
        name="grad_step",
    )(hidden, error, momentum, *tables)


def update_kernel(replicas, bands, row_h, row_l, col_h, col_l, update):
    total = jnp.sum(bands[...].astype(F32), axis=0)
    tile = decode_tile(total, (row_h[...], row_l[...]), (col_h[...], col_l[...]))
    update[...] = (tile * (1.0 / replicas)).astype(BF)


def update_step(bands, tables, units, width):
    replicas, rows_t, kept = bands.shape
    tiles = width // TILE
    whole = lambda a: pl.BlockSpec(a.shape, lambda i: (0, 0))
    return pl.pallas_call(
        functools.partial(update_kernel, replicas),
        grid=(tiles,),
        in_specs=[pl.BlockSpec((replicas, rows_t // tiles, kept), lambda i: (0, i, 0))]
        + [whole(t) for t in tables],
        out_specs=pl.BlockSpec((units, TILE), lambda i: (0, i)),
        out_shape=jax.ShapeDtypeStruct((units, width), BF),
        name="update_step",
    )(bands, *tables)


def make_tables(units):
    return halves(block_table(units // SPAN)) + halves(block_table(TILE // SPAN))


def forward(tokens, target, combine, filled, w_gate, w_up, w_down):
    local_rows = tokens.shape[0]
    piece = lax.all_gather(tokens, "narrow", axis=0, tiled=True)
    gate_proj = jnp.dot(piece, w_gate, preferred_element_type=F32)
    up_proj = jnp.dot(piece, w_up, preferred_element_type=F32)
    hidden = (jax.nn.silu(gate_proj) * up_proj).astype(BF)
    summed = lax.psum_scatter(
        jnp.dot(hidden, w_down, preferred_element_type=F32).astype(BF),
        "narrow",
        scatter_dimension=0,
        tiled=True,
    ).astype(F32)
    weight = combine.astype(F32)[:, None]
    row_ids = lax.axis_index("narrow") * local_rows + jnp.arange(local_rows, dtype=jnp.int32)
    error = jnp.where(
        (row_ids < filled[0])[:, None], weight * (weight * summed - target.astype(F32)), 0.0
    ).astype(BF)
    return hidden, lax.all_gather(error, "narrow", axis=0, tiled=True)


def body(tokens, target, combine, filled, w_gate, w_up, w_down, momentum):
    units, width = w_down.shape
    total_rows = tokens.shape[0] * lax.axis_size("narrow")
    tables = make_tables(units)
    hidden, errors = forward(tokens, target, combine, filled, w_gate, w_up, w_down)
    residue, band = grad_step(hidden, errors, momentum, tables, 1.0 / math.sqrt(total_rows))
    bands = lax.all_gather(band[None], "wide", axis=0, tiled=True)
    return residue, update_step(bands, tables, units, width)


def solution(mesh):
    in_specs = (
        P(("wide", "narrow"), None),
        P(("wide", "narrow"), None),
        P(("wide", "narrow")),
        P("wide"),
        P(None, "narrow"),
        P(None, "narrow"),
        P("narrow", None),
        P("wide", "narrow", None),
    )
    out_specs = (P("wide", "narrow", None), P("narrow", None))
    return jax.shard_map(body, mesh=mesh, in_specs=in_specs, out_specs=out_specs, check_vma=False)
```

```python
import functools
import math

import jax
import jax.numpy as jnp
from jax import lax
from jax.experimental import pallas as pl
from jax.experimental.pallas import tpu as pltpu
from jax.sharding import PartitionSpec as P

SPAN = 64
BAND = 16
TILE = 256
BF = jnp.bfloat16
F32 = jnp.float32


def block_table(blocks):
    shape = (blocks * BAND, blocks * SPAN)
    row = lax.broadcasted_iota(jnp.int32, shape, 0)
    col = lax.broadcasted_iota(jnp.int32, shape, 1)
    freq = (row % BAND).astype(F32)
    cell = (col % SPAN).astype(F32)
    factor = jnp.where(row % BAND == 0, math.sqrt(1.0 / SPAN), math.sqrt(2.0 / SPAN))
    value = factor * jnp.cos(math.pi * (2.0 * cell + 1.0) * freq / (2.0 * SPAN))
    return jnp.where(row // BAND == col // SPAN, value, 0.0)


def halves(value):
    high = value.astype(BF)
    return high, (value - high.astype(F32)).astype(BF)


def dot3(left, right, contract):
    dims = (((contract[0],), (contract[1],)), ((), ()))
    dot = functools.partial(lax.dot_general, dimension_numbers=dims, preferred_element_type=F32)
    return dot(left[0], right[0]) + (dot(left[1], right[0]) + dot(left[0], right[1]))


def decode_tile(band, tables):
    wide = dot3(halves(band), halves(tables[3][...]), (1, 0))
    return dot3(halves(tables[1][...]), halves(wide), (1, 0))


def grad_kernel(factor, hidden_t, error, momentum, *refs):
    tables, (residue, band_t) = refs[:4], refs[4:]
    grad = jnp.dot(hidden_t[...], error[...], preferred_element_type=F32)
    moved = 0.999 * momentum[0] + factor * grad
    squeezed = dot3(halves(tables[0][...]), halves(moved), (1, 0))
    band = dot3(halves(squeezed), halves(tables[2][...]), (1, 0))
    band_t[...] = band.T
    residue[0] = moved - decode_tile(band, tables)


def whole(a):
    return pl.BlockSpec(a.shape, lambda i: (0,) * a.ndim)


def grad_step(hidden_t, error, momentum, tables, factor):
    units, rows = hidden_t.shape
    width = error.shape[1]
    tiles = width // TILE
    kept = units // SPAN * BAND
    kept_t = TILE // SPAN * BAND
    return pl.pallas_call(
        functools.partial(grad_kernel, factor),
        grid=(tiles,),
        in_specs=[
            whole(hidden_t),
            pl.BlockSpec((rows, TILE), lambda i: (0, i)),
            pl.BlockSpec((1, units, TILE), lambda i: (0, 0, i)),
        ]
        + [whole(t) for t in tables],
        out_specs=[
            pl.BlockSpec((1, units, TILE), lambda i: (0, 0, i)),
            pl.BlockSpec((kept_t, kept), lambda i: (i, 0)),
        ],
        out_shape=[
            jax.ShapeDtypeStruct((1, units, width), F32),
            jax.ShapeDtypeStruct((tiles * kept_t, kept), F32),
        ],
        name="grad_step",
    )(hidden_t, error, momentum, *tables)


def update_kernel(replicas, bands, *refs):
    tables, update = refs[:4], refs[4]
    update[...] = (decode_tile(bands[...].T, tables) * (1.0 / replicas)).astype(BF)


def update_step(bands, tables, units, width, replicas):
    rows_t, kept = bands.shape
    tiles = width // TILE
    return pl.pallas_call(
        functools.partial(update_kernel, replicas),
        grid=(tiles,),
        in_specs=[pl.BlockSpec((rows_t // tiles, kept), lambda i: (i, 0))]
        + [whole(t) for t in tables],
        out_specs=pl.BlockSpec((units, TILE), lambda i: (0, i)),
        out_shape=jax.ShapeDtypeStruct((units, width), BF),
        name="update_step",
    )(bands, *tables)


def make_tables(units):
    left = block_table(units // SPAN)
    right = block_table(TILE // SPAN)
    return left, left.T, right.T, right


def remote(src, dst, send, recv, index, axis, peer):
    return pltpu.make_async_remote_copy(
        src_ref=src,
        dst_ref=dst,
        send_sem=send.at[index],
        recv_sem=recv.at[index],
        device_id={axis: peer},
        device_id_type=pl.DeviceIdType.MESH,
    )


def greet(axis, peers):
    barrier = pltpu.get_barrier_semaphore()
    for peer in peers:
        pl.semaphore_signal(
            barrier, inc=1, device_id={axis: peer}, device_id_type=pl.DeviceIdType.MESH
        )
    pl.semaphore_wait(barrier, len(peers))


def square_kernel(
    tokens, target, weight, live, gate_hbm, up_hbm, down_hbm, hidden_out, error_out,
    gate, up, down, held, part, errors, from_x, from_y, relay_x, relay_y, hidden_t, hidden,
    send, recv, local,
):
    me = lax.axis_index("narrow")
    x_peer = me + 1 - 2 * (me % 2)
    y_peer = (me + 2) % 4
    rows, width = tokens.shape
    units = down.shape[0]
    half = rows // 2
    top, low = pl.ds(0, half), pl.ds(half, half)

    loads = [
        pltpu.make_async_copy(s, t, local.at[i])
        for i, (s, t) in enumerate(((gate_hbm, gate), (up_hbm, up), (down_hbm, down)))
    ]
    for load in loads:
        load.start()
    greet("narrow", (x_peer, y_peer))

    def spread(own, slots, base):
        copies = [
            remote(own.at[top], slots.at[0, top], send, recv, base, "narrow", x_peer),
            remote(own.at[low], slots.at[1, low], send, recv, base + 1, "narrow", y_peer),
            remote(own.at[low], slots.at[0, low], send, recv, base + 2, "narrow", x_peer),
            remote(own.at[top], slots.at[1, top], send, recv, base + 3, "narrow", y_peer),
            remote(slots.at[0, top], slots.at[2, top], send, recv, base + 4, "narrow", y_peer),
            remote(slots.at[1, low], slots.at[2, low], send, recv, base + 5, "narrow", x_peer),
        ]
        for copy in copies[:4]:
            copy.start()
        return copies

    def pass_on(copies):
        copies[0].wait_recv()
        copies[4].start()
        copies[1].wait_recv()
        copies[5].start()

    def expert(source, slot):
        @pl.loop(0, units // TILE)
        def _(c):
            at = pl.ds(pl.multiple_of(c * TILE, TILE), TILE)
            block = source[...]
            gated = jnp.dot(block, gate[:, at], preferred_element_type=F32)
            raised = jnp.dot(block, up[:, at], preferred_element_type=F32)
            value = gated / (1.0 + jnp.exp(-gated)) * raised
            hidden[:, at] = value.astype(BF)
            hidden_t[at, slot * rows : (slot + 1) * rows] = value.T.astype(BF)

        @pl.loop(0, width // TILE)
        def _(c):
            at = pl.ds(pl.multiple_of(c * TILE, TILE), TILE)
            part[slot, :, at] = jnp.dot(
                hidden[...], down[:, at], preferred_element_type=F32
            ).astype(BF)

    gathers = spread(tokens, held, 0)
    for load in loads:
        load.wait()
    expert(tokens, 0)
    pass_on(gathers)
    gathers[2].wait_recv()
    expert(held.at[0], 1)
    sums = [
        remote(part.at[3, top], relay_y, send, recv, 6, "narrow", x_peer),
        remote(part.at[3, low], relay_x, send, recv, 7, "narrow", y_peer),
        remote(part.at[1, top], from_x.at[top], send, recv, 8, "narrow", x_peer),
        remote(part.at[2, low], from_y.at[low], send, recv, 9, "narrow", y_peer),
        remote(part.at[1, low], from_x.at[low], send, recv, 10, "narrow", x_peer),
        remote(part.at[2, top], from_y.at[top], send, recv, 11, "narrow", y_peer),
    ]
    sums[2].start()
    gathers[3].wait_recv()
    expert(held.at[1], 2)
    sums[3].start()
    gathers[4].wait_recv()
    gathers[5].wait_recv()
    expert(held.at[2], 3)
    sums[0].start()
    sums[1].start()
    hidden_store = pltpu.make_async_copy(hidden_t, hidden_out, local.at[3])
    hidden_store.start()

    step = 16

    def add_rows(slot, first, arrived):
        @pl.loop(0, half // step)
        def _(c):
            mine = pl.ds(pl.multiple_of(first + c * step, step), step)
            theirs = pl.ds(pl.multiple_of(c * step, step), step)
            part[slot, mine, :] = (
                part[slot, mine, :].astype(F32) + arrived[theirs, :].astype(F32)
            ).astype(BF)

    def error_rows(first):
        @pl.loop(0, half // step)
        def _(c):
            at = pl.ds(pl.multiple_of(first + c * step, step), step)
            total = (
                part[0, at, :].astype(F32)
                + from_x[at, :].astype(F32)
                + from_y[at, :].astype(F32)
            )
            scale = weight[at, :]
            value = scale * (scale * total - target[at, :].astype(F32))
            errors[0, at, :] = jnp.where(live[at, :] > 0.0, value, 0.0).astype(BF)

    sums[0].wait_recv()
    add_rows(2, 0, relay_y)
    sums[5].start()
    sums[1].wait_recv()
    add_rows(1, half, relay_x)
    sums[4].start()
    sums[2].wait_recv()
    sums[5].wait_recv()
    error_rows(0)
    sums[3].wait_recv()
    sums[4].wait_recv()
    error_rows(half)
    shared = spread(errors.at[0], errors.at[pl.ds(1, 3)], 12)
    stores = [
        pltpu.make_async_copy(errors.at[i], error_out.at[i], local.at[4 + i]) for i in range(4)
    ]
    stores[0].start()
    pass_on(shared)
    shared[2].wait_recv()
    stores[1].start()
    shared[3].wait_recv()
    stores[2].start()
    shared[4].wait_recv()
    shared[5].wait_recv()
    stores[3].start()
    for copy in gathers + sums + shared:
        copy.wait_send()
    hidden_store.wait()
    for store in stores:
        store.wait()


def square_forward(tokens, target, combine, filled, w_gate, w_up, w_down):
    rows, width = tokens.shape
    units = w_down.shape[0]
    half = rows // 2
    row_ids = lax.axis_index("narrow") * rows + jnp.arange(rows, dtype=jnp.int32)
    live = (row_ids < filled[0]).astype(F32)[:, None]
    weight = combine.astype(F32)[:, None]
    vmem = pl.BlockSpec(memory_space=pltpu.VMEM)
    hbm = pl.BlockSpec(memory_space=pl.ANY)
    block = lambda *shape: pltpu.VMEM(shape, BF)
    hidden_t, errors = pl.pallas_call(
        square_kernel,
        in_specs=[vmem] * 4 + [hbm] * 3,
        out_specs=[hbm] * 2,
        out_shape=[
            jax.ShapeDtypeStruct((units, 4 * rows), BF),
            jax.ShapeDtypeStruct((4, rows, width), BF),
        ],
        scratch_shapes=[
            block(width, units), block(width, units), block(units, width),
            block(3, rows, width), block(4, rows, width), block(4, rows, width),
            block(rows, width), block(rows, width), block(half, width), block(half, width),
            block(units, 4 * rows), block(rows, units),
            pltpu.SemaphoreType.DMA((18,)), pltpu.SemaphoreType.DMA((18,)),
            pltpu.SemaphoreType.DMA((8,)),
        ],
        compiler_params=pltpu.CompilerParams(
            collective_id=0, has_side_effects=True, vmem_limit_bytes=60 << 20
        ),
        name="square_forward",
    )(tokens, target, weight, live, w_gate, w_up, w_down)
    return hidden_t, errors.reshape(4 * rows, width)


def band_kernel(count, band, total, outgoing, arrived, summed, gathered, send, recv):
    me = lax.axis_index("wide")
    peers = [(me + k) % count for k in range(1, count)]
    greet("wide", peers)
    share = band.shape[0] // count
    outgoing[...] = band[...].reshape(count, share, band.shape[1]).astype(BF)
    first = [
        remote(outgoing.at[p], arrived.at[k], send, recv, k, "wide", p)
        for k, p in enumerate(peers)
    ]
    for copy in first:
        copy.start()
    amount = outgoing[me].astype(F32)
    for k, copy in enumerate(first):
        copy.wait_recv()
        amount = amount + arrived[k].astype(F32)
    summed[...] = amount.astype(BF)
    second = [
        remote(summed, gathered.at[me], send, recv, count + k, "wide", p)
        for k, p in enumerate(peers)
    ]
    for copy in second:
        copy.start()
    for copy in second:
        copy.wait_recv()
    for copy in first + second:
        copy.wait_send()
    gathered[me] = summed[...]
    total[...] = gathered[...].astype(F32).reshape(band.shape)


def band_sum(band, count):
    share = band.shape[0] // count
    vmem = pl.BlockSpec(memory_space=pltpu.VMEM)
    block = lambda *shape: pltpu.VMEM(shape + (share, band.shape[1]), BF)
    return pl.pallas_call(
        functools.partial(band_kernel, count),
        in_specs=[vmem],
        out_specs=vmem,
        out_shape=jax.ShapeDtypeStruct(band.shape, F32),
        scratch_shapes=[
            block(count), block(count - 1), block(), block(count),
            pltpu.SemaphoreType.DMA((2 * count,)), pltpu.SemaphoreType.DMA((2 * count,)),
        ],
        compiler_params=pltpu.CompilerParams(collective_id=1, has_side_effects=True),
        name="band_sum",
    )(band)


def forward(tokens, target, combine, filled, w_gate, w_up, w_down):
    local_rows = tokens.shape[0]
    piece = lax.all_gather(tokens, "narrow", axis=0, tiled=True)
    gate_proj = jnp.dot(piece, w_gate, preferred_element_type=F32)
    up_proj = jnp.dot(piece, w_up, preferred_element_type=F32)
    hidden = (jax.nn.silu(gate_proj) * up_proj).astype(BF)
    summed = lax.psum_scatter(
        jnp.dot(hidden, w_down, preferred_element_type=F32).astype(BF),
        "narrow",
        scatter_dimension=0,
        tiled=True,
    ).astype(F32)
    weight = combine.astype(F32)[:, None]
    row_ids = lax.axis_index("narrow") * local_rows + jnp.arange(local_rows, dtype=jnp.int32)
    error = jnp.where(
        (row_ids < filled[0])[:, None], weight * (weight * summed - target.astype(F32)), 0.0
    ).astype(BF)
    return hidden.T, lax.all_gather(error, "narrow", axis=0, tiled=True)


def body(tokens, target, combine, filled, w_gate, w_up, w_down, momentum):
    units, width = w_down.shape
    narrow, replicas = lax.axis_size("narrow"), lax.axis_size("wide")
    total_rows = tokens.shape[0] * narrow
    tables = make_tables(units)
    step = square_forward if narrow == 4 else forward
    hidden_t, errors = step(tokens, target, combine, filled, w_gate, w_up, w_down)
    residue, band = grad_step(hidden_t, errors, momentum, tables, 1.0 / math.sqrt(total_rows))
    if narrow == 4:
        total = band_sum(band, replicas)
    else:
        bands = lax.all_gather(band.astype(BF)[None], "wide", axis=0, tiled=True)
        total = jnp.sum(bands.astype(F32), axis=0)
    return residue, update_step(total, tables, units, width, replicas)


def solution(mesh):
    in_specs = (
        P(("wide", "narrow"), None),
        P(("wide", "narrow"), None),
        P(("wide", "narrow")),
        P("wide"),
        P(None, "narrow"),
        P(None, "narrow"),
        P("narrow", None),
        P("wide", "narrow", None),
    )
    out_specs = (P("wide", "narrow", None), P("narrow", None))
    return jax.shard_map(body, mesh=mesh, in_specs=in_specs, out_specs=out_specs, check_vma=False)
```

```python
import functools
import math

import jax
import jax.numpy as jnp
import numpy as np
from jax import lax
from jax.experimental import pallas as pl
from jax.experimental.pallas import tpu as pltpu
from jax.sharding import PartitionSpec as P

SPAN = 64
BAND = 16
TILE = 256
BF = jnp.bfloat16
F32 = jnp.float32


def block_table(blocks):
    row = np.arange(blocks * BAND)[:, None]
    col = np.arange(blocks * SPAN)[None, :]
    factor = np.where(row % BAND == 0, math.sqrt(1.0 / SPAN), math.sqrt(2.0 / SPAN))
    value = factor * np.cos(math.pi * (2.0 * (col % SPAN) + 1.0) * (row % BAND) / (2.0 * SPAN))
    return np.where(row // BAND == col // SPAN, value, 0.0).astype(np.float32)


def halves(value):
    high = value.astype(BF)
    return high, (value - high.astype(F32)).astype(BF)


def dot3(left, right, contract):
    dims = (((contract[0],), (contract[1],)), ((), ()))
    dot = functools.partial(lax.dot_general, dimension_numbers=dims, preferred_element_type=F32)
    return dot(left[0], right[0]) + (dot(left[1], right[0]) + dot(left[0], right[1]))


def decode_tile(band, tables):
    wide = dot3(halves(band), tables[3], (1, 0))
    return dot3(tables[1], halves(wide), (1, 0))


def read_tables(refs):
    return [(refs[2 * k][...], refs[2 * k + 1][...]) for k in range(4)]


def grad_kernel(factor, subs, hidden_t, error, momentum, *refs):
    residue, band_t = refs[8:]
    tables = read_tables(refs)
    kept_t = TILE // SPAN * BAND
    for k in range(subs):
        at = slice(k * TILE, (k + 1) * TILE)
        grad = jnp.dot(hidden_t[...], error[:, at], preferred_element_type=F32)
        moved = 0.999 * momentum[0, :, at] + factor * grad
        squeezed = dot3(tables[0], halves(moved), (1, 0))
        band = dot3(halves(squeezed), tables[2], (1, 0))
        band_t[k * kept_t : (k + 1) * kept_t, :] = band.T
        residue[0, :, at] = moved - decode_tile(band, tables)


def whole(a):
    return pl.BlockSpec(a.shape, lambda i: (0,) * a.ndim)


def grad_step(hidden_t, error, momentum, tables, factor):
    units, rows = hidden_t.shape
    width = error.shape[1]
    subs = 3 if width // TILE % 3 == 0 else 1
    step = TILE * subs
    tiles = width // step
    kept = units // SPAN * BAND
    kept_t = step // SPAN * BAND
    return pl.pallas_call(
        functools.partial(grad_kernel, factor, subs),
        grid=(tiles,),
        in_specs=[
            whole(hidden_t),
            pl.BlockSpec((rows, step), lambda i: (0, i)),
            pl.BlockSpec((1, units, step), lambda i: (0, 0, i)),
        ]
        + [whole(t) for t in tables],
        out_specs=[
            pl.BlockSpec((1, units, step), lambda i: (0, 0, i)),
            pl.BlockSpec((kept_t, kept), lambda i: (i, 0)),
        ],
        out_shape=[
            jax.ShapeDtypeStruct((1, units, width), F32),
            jax.ShapeDtypeStruct((tiles * kept_t, kept), F32),
        ],
        name="grad_step",
    )(hidden_t, error, momentum, *tables)


def update_kernel(replicas, subs, bands, *refs):
    update = refs[8]
    tables = read_tables(refs)
    kept_t = TILE // SPAN * BAND
    for k in range(subs):
        band = bands[k * kept_t : (k + 1) * kept_t, :].T
        tile = decode_tile(band, tables) * (1.0 / replicas)
        update[:, k * TILE : (k + 1) * TILE] = tile.astype(BF)


def update_step(bands, tables, units, width, replicas):
    rows_t, kept = bands.shape
    subs = 3 if width // TILE % 3 == 0 else 1
    step = TILE * subs
    tiles = width // step
    return pl.pallas_call(
        functools.partial(update_kernel, replicas, subs),
        grid=(tiles,),
        in_specs=[pl.BlockSpec((rows_t // tiles, kept), lambda i: (i, 0))]
        + [whole(t) for t in tables],
        out_specs=pl.BlockSpec((units, step), lambda i: (0, i)),
        out_shape=jax.ShapeDtypeStruct((units, width), BF),
        name="update_step",
    )(bands, *tables)


def make_tables(units):
    left = block_table(units // SPAN)
    right = block_table(TILE // SPAN)
    pieces = []
    for table in (left, left.T, right.T, right):
        high = table.astype(BF)
        pieces += [high, (table - high.astype(np.float32)).astype(BF)]
    return [jnp.asarray(np.ascontiguousarray(p)) for p in pieces]


def remote(src, dst, send, recv, index, axis, peer):
    return pltpu.make_async_remote_copy(
        src_ref=src,
        dst_ref=dst,
        send_sem=send.at[index],
        recv_sem=recv.at[index],
        device_id={axis: peer},
        device_id_type=pl.DeviceIdType.MESH,
    )


def greet(axis, peers):
    barrier = pltpu.get_barrier_semaphore()
    for peer in peers:
        pl.semaphore_signal(
            barrier, inc=1, device_id={axis: peer}, device_id_type=pl.DeviceIdType.MESH
        )
    pl.semaphore_wait(barrier, len(peers))


def square_kernel(
    tokens, target, weight, gate_hbm, up_hbm, down_hbm, hidden_out, error_out,
    gate, up, down, held, part, errors, from_x, from_y, relay_x, relay_y, hidden_t, hidden,
    send, recv, local,
):
    me = lax.axis_index("narrow")
    x_peer = me + 1 - 2 * (me % 2)
    y_peer = (me + 2) % 4
    rows, width = tokens.shape
    units = down.shape[0]
    half = rows // 2
    top, low = pl.ds(0, half), pl.ds(half, half)

    loads = [
        pltpu.make_async_copy(s, t, local.at[i])
        for i, (s, t) in enumerate(((gate_hbm, gate), (up_hbm, up), (down_hbm, down)))
    ]
    for load in loads:
        load.start()
    greet("narrow", (x_peer, y_peer))

    def spread(own, slots, base):
        copies = [
            remote(own.at[top], slots.at[0, top], send, recv, base, "narrow", x_peer),
            remote(own.at[low], slots.at[1, low], send, recv, base + 1, "narrow", y_peer),
            remote(own.at[low], slots.at[0, low], send, recv, base + 2, "narrow", x_peer),
            remote(own.at[top], slots.at[1, top], send, recv, base + 3, "narrow", y_peer),
            remote(slots.at[0, top], slots.at[2, top], send, recv, base + 4, "narrow", y_peer),
            remote(slots.at[1, low], slots.at[2, low], send, recv, base + 5, "narrow", x_peer),
        ]
        for copy in copies[:4]:
            copy.start()
        return copies

    def pass_on(copies):
        copies[0].wait_recv()
        copies[4].start()
        copies[1].wait_recv()
        copies[5].start()

    def expert(source, slot):
        @pl.loop(0, units // TILE)
        def _(c):
            at = pl.ds(pl.multiple_of(c * TILE, TILE), TILE)
            block = source[...]
            gated = jnp.dot(block, gate[:, at], preferred_element_type=F32)
            raised = jnp.dot(block, up[:, at], preferred_element_type=F32)
            value = gated / (1.0 + jnp.exp(-gated)) * raised
            hidden[:, at] = value.astype(BF)
            hidden_t[at, slot * rows : (slot + 1) * rows] = value.T.astype(BF)

        @pl.loop(0, width // TILE)
        def _(c):
            at = pl.ds(pl.multiple_of(c * TILE, TILE), TILE)
            part[slot, :, at] = jnp.dot(
                hidden[...], down[:, at], preferred_element_type=F32
            ).astype(BF)

    gathers = spread(tokens, held, 0)
    for load in loads:
        load.wait()
    expert(tokens, 0)
    pass_on(gathers)
    gathers[2].wait_recv()
    expert(held.at[0], 1)
    sums = [
        remote(part.at[3, top], relay_y, send, recv, 6, "narrow", x_peer),
        remote(part.at[3, low], relay_x, send, recv, 7, "narrow", y_peer),
        remote(part.at[1, top], from_x.at[top], send, recv, 8, "narrow", x_peer),
        remote(part.at[2, low], from_y.at[low], send, recv, 9, "narrow", y_peer),
        remote(part.at[1, low], from_x.at[low], send, recv, 10, "narrow", x_peer),
        remote(part.at[2, top], from_y.at[top], send, recv, 11, "narrow", y_peer),
    ]
    sums[2].start()
    gathers[3].wait_recv()
    expert(held.at[1], 2)
    sums[3].start()
    gathers[4].wait_recv()
    gathers[5].wait_recv()
    expert(held.at[2], 3)
    sums[0].start()
    sums[1].start()
    hidden_store = pltpu.make_async_copy(hidden_t, hidden_out, local.at[3])
    hidden_store.start()

    step = 16

    def add_rows(slot, first, arrived):
        @pl.loop(0, half // step)
        def _(c):
            mine = pl.ds(pl.multiple_of(first + c * step, step), step)
            theirs = pl.ds(pl.multiple_of(c * step, step), step)
            part[slot, mine, :] = (
                part[slot, mine, :].astype(F32) + arrived[theirs, :].astype(F32)
            ).astype(BF)

    def error_rows(first):
        @pl.loop(0, half // step)
        def _(c):
            at = pl.ds(pl.multiple_of(first + c * step, step), step)
            total = (
                part[0, at, :].astype(F32)
                + from_x[at, :].astype(F32)
                + from_y[at, :].astype(F32)
            )
            scale = weight[at, :]
            value = scale * (scale * total - target[at, :].astype(F32))
            errors[0, at, :] = value.astype(BF)

    sums[0].wait_recv()
    add_rows(2, 0, relay_y)
    sums[5].start()
    sums[1].wait_recv()
    add_rows(1, half, relay_x)
    sums[4].start()
    sums[2].wait_recv()
    sums[5].wait_recv()
    error_rows(0)
    sums[3].wait_recv()
    sums[4].wait_recv()
    error_rows(half)
    shared = spread(errors.at[0], errors.at[pl.ds(1, 3)], 12)
    stores = [
        pltpu.make_async_copy(errors.at[i], error_out.at[i], local.at[4 + i]) for i in range(4)
    ]
    stores[0].start()
    pass_on(shared)
    shared[2].wait_recv()
    stores[1].start()
    shared[3].wait_recv()
    stores[2].start()
    shared[4].wait_recv()
    shared[5].wait_recv()
    stores[3].start()
    for copy in gathers + sums + shared:
        copy.wait_send()
    hidden_store.wait()
    for store in stores:
        store.wait()


def square_forward(tokens, target, combine, filled, w_gate, w_up, w_down):
    rows, width = tokens.shape
    units = w_down.shape[0]
    half = rows // 2
    row_ids = lax.axis_index("narrow") * rows + jnp.arange(rows, dtype=jnp.int32)
    weight = jnp.where(row_ids < filled[0], combine.astype(F32), 0.0)[:, None]
    vmem = pl.BlockSpec(memory_space=pltpu.VMEM)
    hbm = pl.BlockSpec(memory_space=pl.ANY)
    block = lambda *shape: pltpu.VMEM(shape, BF)
    hidden_t, errors = pl.pallas_call(
        square_kernel,
        in_specs=[vmem] * 3 + [hbm] * 3,
        out_specs=[hbm] * 2,
        out_shape=[
            jax.ShapeDtypeStruct((units, 4 * rows), BF),
            jax.ShapeDtypeStruct((4, rows, width), BF),
        ],
        scratch_shapes=[
            block(width, units), block(width, units), block(units, width),
            block(3, rows, width), block(4, rows, width), block(4, rows, width),
            block(rows, width), block(rows, width), block(half, width), block(half, width),
            block(units, 4 * rows), block(rows, units),
            pltpu.SemaphoreType.DMA((18,)), pltpu.SemaphoreType.DMA((18,)),
            pltpu.SemaphoreType.DMA((8,)),
        ],
        compiler_params=pltpu.CompilerParams(
            collective_id=0, has_side_effects=True, vmem_limit_bytes=60 << 20
        ),
        name="square_forward",
    )(tokens, target, weight, w_gate, w_up, w_down)
    return hidden_t, errors.reshape(4 * rows, width)


def band_kernel(count, band, total, outgoing, arrived, summed, gathered, send, recv):
    me = lax.axis_index("wide")
    peers = [(me + k) % count for k in range(1, count)]
    greet("wide", peers)
    share = band.shape[0] // count
    outgoing[...] = band[...].reshape(count, share, band.shape[1]).astype(BF)
    first = [
        remote(outgoing.at[p], arrived.at[k], send, recv, k, "wide", p)
        for k, p in enumerate(peers)
    ]
    for copy in first:
        copy.start()
    amount = outgoing[me].astype(F32)
    for k, copy in enumerate(first):
        copy.wait_recv()
        amount = amount + arrived[k].astype(F32)
    summed[...] = amount.astype(BF)
    second = [
        remote(summed, gathered.at[me], send, recv, count + k, "wide", p)
        for k, p in enumerate(peers)
    ]
    for copy in second:
        copy.start()
    for copy in second:
        copy.wait_recv()
    for copy in first + second:
        copy.wait_send()
    gathered[me] = summed[...]
    total[...] = gathered[...].astype(F32).reshape(band.shape)


def band_sum(band, count):
    share = band.shape[0] // count
    vmem = pl.BlockSpec(memory_space=pltpu.VMEM)
    block = lambda *shape: pltpu.VMEM(shape + (share, band.shape[1]), BF)
    return pl.pallas_call(
        functools.partial(band_kernel, count),
        in_specs=[vmem],
        out_specs=vmem,
        out_shape=jax.ShapeDtypeStruct(band.shape, F32),
        scratch_shapes=[
            block(count), block(count - 1), block(), block(count),
            pltpu.SemaphoreType.DMA((2 * count,)), pltpu.SemaphoreType.DMA((2 * count,)),
        ],
        compiler_params=pltpu.CompilerParams(collective_id=1, has_side_effects=True),
        name="band_sum",
    )(band)


def forward(tokens, target, combine, filled, w_gate, w_up, w_down):
    local_rows = tokens.shape[0]
    piece = lax.all_gather(tokens, "narrow", axis=0, tiled=True)
    gate_proj = jnp.dot(piece, w_gate, preferred_element_type=F32)
    up_proj = jnp.dot(piece, w_up, preferred_element_type=F32)
    hidden = (jax.nn.silu(gate_proj) * up_proj).astype(BF)
    summed = lax.psum_scatter(
        jnp.dot(hidden, w_down, preferred_element_type=F32).astype(BF),
        "narrow",
        scatter_dimension=0,
        tiled=True,
    ).astype(F32)
    weight = combine.astype(F32)[:, None]
    row_ids = lax.axis_index("narrow") * local_rows + jnp.arange(local_rows, dtype=jnp.int32)
    error = jnp.where(
        (row_ids < filled[0])[:, None], weight * (weight * summed - target.astype(F32)), 0.0
    ).astype(BF)
    return hidden.T, lax.all_gather(error, "narrow", axis=0, tiled=True)


def body(tokens, target, combine, filled, w_gate, w_up, w_down, momentum):
    units, width = w_down.shape
    narrow, replicas = lax.axis_size("narrow"), lax.axis_size("wide")
    total_rows = tokens.shape[0] * narrow
    tables = make_tables(units)
    step = square_forward if narrow == 4 else forward
    hidden_t, errors = step(tokens, target, combine, filled, w_gate, w_up, w_down)
    residue, band = grad_step(hidden_t, errors, momentum, tables, 1.0 / math.sqrt(total_rows))
    if narrow == 4:
        total = band_sum(band, replicas)
    else:
        bands = lax.all_gather(band.astype(BF)[None], "wide", axis=0, tiled=True)
        total = jnp.sum(bands.astype(F32), axis=0)
    return residue, update_step(total, tables, units, width, replicas)


def solution(mesh):
    in_specs = (
        P(("wide", "narrow"), None),
        P(("wide", "narrow"), None),
        P(("wide", "narrow")),
        P("wide"),
        P(None, "narrow"),
        P(None, "narrow"),
        P("narrow", None),
        P("wide", "narrow", None),
    )
    out_specs = (P("wide", "narrow", None), P("narrow", None))
    return jax.shard_map(body, mesh=mesh, in_specs=in_specs, out_specs=out_specs, check_vma=False)
```
